512 devices in a mesh: gx: 8 (over z_lo), gy: 8 (over y, z_hi), gz: 8 (over x, core).
Axes of the slice: x: 4, y: 4, z: 16 (z_hi: 2, z_lo: 8; z = z_hi * 8 + z_lo), core: 2. Of those that a mesh axis runs over, the one named last changes fastest.
Arguments:
- state_send: float32 [13, 216, 65536], P(None, None, ('gx', 'gy', 'gz')), may hold values from -0.5 to 14, as said below
- order_send: int32 [65536], P(('gx', 'gy', 'gz')), may hold values from 1 to 5
- send_count: int32 [512, 64], P(('gx', 'gy', 'gz')), may hold values from 0 to 2, as said below
- neighbours: int32 [6, 65536], P(None, ('gx', 'gy', 'gz')), may hold values from 0 to 159, as said below
Outputs:
- new_state: float32 [13, 216, 65536], P(None, None, ('gx', 'gy', 'gz'))
The draws below stay inside these ranges and needn't reach their ends.
Inputs may be any that keep to these rules, and one draw needn't show every extreme that they name: `state_send`: rows 0 to 8 are species densities in [0.005, 2], rows 9 to 11 momenta in [-0.5, 0.5], row 12 total energy in [3, 14], with energy above 0.5 |momentum|^2 / density at every node. `send_count`: in every draw one receiver of each gx index gets 2 elements from every device of that index. `neighbours`: every face of a live new element names a live element; faces 0, 2, 4 of slots below 16 may name the previous device's last 16 slots, faces 1, 3, 5 of the last 16 slots the next device's first 16; the first device has no previous and the last no next; empty slots name themselves.
All inputs are finite; a program needn't handle non-finite values.
Results may differ from the reference program's by a relative error of at most 0.0003.
Values sent between devices are 32-bit elements; how exact they have to be, the bound alone decides.
No kernel may reach another device: no remote copies, remote signals or barrier semaphores. Data moves between devices by JAX's collectives and lax.ppermute only.
A program may use at most 128 MiB of HBM per device.

```python
import math
import jax
import jax.numpy as jnp
import numpy as np
from jax import lax

NV = 13
PMAX = 5
NODES = 216
BAND = 16
SLOTS = 128
PEERS = 64
CAP = 2
ELEMENTS = 65536
DEVICES = 512


def shared_counts(key):
    base_key = jax.random.fold_in(key, 7)
    counts = jax.random.randint(jax.random.fold_in(base_key, 1), (DEVICES, PEERS), 0, CAP + 1)
    full_peer = jax.random.randint(jax.random.fold_in(base_key, 2), (DEVICES // PEERS,), 0, PEERS)
    target = full_peer[jnp.arange(DEVICES) // PEERS]
    counts = jnp.where(jnp.arange(PEERS)[None, :] == target[:, None], CAP, counts)
    return counts.astype(jnp.int32)


def draw_send_count(key, part):
    return shared_counts(key)


def draw_neighbours(key, part):
    counts = shared_counts(key)
    groups = DEVICES // PEERS
    by_receiver = counts.reshape(groups, PEERS, PEERS).transpose(0, 2, 1).reshape(DEVICES, PEERS)
    positions = jnp.arange(SLOTS)
    is_live = (positions % CAP)[None, :] < by_receiver[:, positions // CAP]
    first_live = jnp.argmax(is_live.astype(jnp.int32), axis=1)
    key_one = jax.random.fold_in(key, 11)
    key_two = jax.random.fold_in(key, 12)
    key_three = jax.random.fold_in(key, 13)
    candidate = jax.random.randint(key_one, (6, DEVICES, SLOTS), 0, SLOTS)
    live_wide = jnp.broadcast_to(is_live[None], (6, DEVICES, SLOTS))
    cand_live = jnp.take_along_axis(live_wide, candidate, axis=2)
    local_pick = jnp.where(cand_live, candidate, first_live[None, :, None]) + BAND
    remote_roll = jax.random.randint(key_two, (6, DEVICES, SLOTS), 0, 4) == 0
    band_pick = jax.random.randint(key_three, (6, DEVICES, SLOTS), 0, BAND)
    empty_row = jnp.zeros((1, SLOTS), dtype=bool)
    live_prev = jnp.concatenate([empty_row, is_live[:-1]], axis=0)
    live_next = jnp.concatenate([is_live[1:], empty_row], axis=0)
    prev_ok = jnp.take_along_axis(jnp.broadcast_to(live_prev[None], (6, DEVICES, SLOTS)), SLOTS - BAND + band_pick, axis=2)
    next_ok = jnp.take_along_axis(jnp.broadcast_to(live_next[None], (6, DEVICES, SLOTS)), band_pick, axis=2)
    face_even = (jnp.arange(6) % 2 == 0)[:, None, None]
    low_band = (positions < BAND)[None, None, :]
    high_band = (positions >= SLOTS - BAND)[None, None, :]
    use_prev = face_even & low_band & remote_roll & prev_ok
    use_next = ~face_even & high_band & remote_roll & next_ok
    links = jnp.where(use_prev, band_pick, jnp.where(use_next, BAND + SLOTS + band_pick, local_pick))
    links = jnp.where(is_live[None], links, BAND + positions[None, None, :])
    return links.reshape(6, DEVICES * SLOTS).astype(jnp.int32)


def draw_state_send(key, part):
    total = DEVICES * SLOTS
    key_one = jax.random.fold_in(key, 21)
    key_two = jax.random.fold_in(key, 22)
    key_three = jax.random.fold_in(key, 23)
    species = jnp.exp(jax.random.uniform(key_one, (9, NODES, total), jnp.float32, math.log(0.02), 0.0))
    momentum = jnp.clip(0.2 * jax.random.normal(key_two, (3, NODES, total), jnp.float32), -0.5, 0.5)
    energy = jax.random.uniform(key_three, (1, NODES, total), jnp.float32, 3.0, 6.0)
    return jnp.concatenate([species, momentum, energy], axis=0).astype(jnp.float32)


def with_ends(entries, own_key, least, largest):
    longest = entries.shape.index(max(entries.shape))
    spots = []
    for shift in (0, 1):
        where = [jax.random.randint(jax.random.fold_in(own_key, axis), (), 0, length) for axis, length in enumerate(entries.shape)]
        where[longest] = (where[longest] + shift) % entries.shape[longest]
        spots.append(tuple(where))
    return entries.at[spots[0]].set(least).at[spots[1]].set(largest)


def setup_inputs(seed: int = 0) -> dict:
    keys = jax.random.split(jax.random.key(seed), 5)
    state_send = draw_state_send(jax.random.fold_in(keys[4], 71), 0)
    order_send = with_ends(jax.random.randint(keys[1], (ELEMENTS,), 1, PMAX + 1), jax.random.fold_in(keys[1], 1), 1, PMAX).astype(jnp.int32)
    send_count = draw_send_count(jax.random.fold_in(keys[4], 71), 0)
    neighbours = draw_neighbours(jax.random.fold_in(keys[4], 71), 0)
    return dict(state_send=state_send, order_send=order_send, send_count=send_count, neighbours=neighbours)


step_scale = 0.02
positivity_eps = 0.001
floor_gap = 0.05

def lagrange_coeffs(node_pos, column):
    coeffs = [1.0]
    denom = 1.0
    for other in range(len(node_pos)):
        if other == column:
            continue
        shifted = [0.0] * (len(coeffs) + 1)
        for power in range(len(coeffs)):
            shifted[power + 1] += coeffs[power]
            shifted[power] -= float(node_pos[other]) * coeffs[power]
        coeffs = shifted
        denom = denom * (float(node_pos[column]) - float(node_pos[other]))
    return [value / denom for value in coeffs]

def poly_value(coeffs, point):
    total = 0.0
    for power in range(len(coeffs)):
        total += coeffs[power] * point ** power
    return total

def poly_slope(coeffs, point):
    total = 0.0
    for power in range(1, len(coeffs)):
        total += power * coeffs[power] * point ** (power - 1)
    return total

def poly_integral(coeffs):
    total = 0.0
    for power in range(len(coeffs)):
        total += coeffs[power] * (1.0 - (-1.0) ** (power + 1)) / (power + 1)
    return total

def basis_tables():
    points = PMAX + 1
    common = np.linspace(-1.0, 1.0, points)
    derivs = np.zeros((PMAX, points, points))
    weights = np.zeros((PMAX, points))
    inverse = np.zeros((PMAX, points))
    interp = np.zeros((PMAX, points, points))
    for degree in range(1, PMAX + 1):
        node_pos = np.linspace(-1.0, 1.0, degree + 1)
        for column in range(degree + 1):
            coeffs = lagrange_coeffs(node_pos, column)
            weights[degree - 1, column] = poly_integral(coeffs)
            for row in range(points):
                interp[degree - 1, row, column] = poly_value(coeffs, float(common[row]))
            for row in range(degree + 1):
                derivs[degree - 1, row, column] = poly_slope(coeffs, float(node_pos[row]))
        inverse[degree - 1, :degree + 1] = 1.0 / weights[degree - 1, :degree + 1]
    return (derivs, weights, inverse, interp, weights[PMAX - 1].copy())

def selections(degree):
    points = PMAX + 1
    derivs, weights, inverse, interp, common_w = basis_tables()
    highest = lax.Precision.HIGHEST
    levels = jnp.arange(1, PMAX + 1, dtype=jnp.int32)
    onehot = (degree[None, :] == levels[:, None]).astype(jnp.float32)
    deriv_sel = jnp.einsum('pij,pe->ije', jnp.asarray(derivs, jnp.float32), onehot, precision=highest)
    weight_sel = jnp.einsum('pi,pe->ie', jnp.asarray(weights, jnp.float32), onehot, precision=highest)
    inverse_sel = jnp.einsum('pi,pe->ie', jnp.asarray(inverse, jnp.float32), onehot, precision=highest)
    interp_sel = jnp.einsum('pqj,pe->qje', jnp.asarray(interp, jnp.float32), onehot, precision=highest)
    weighted_interp = interp_sel * jnp.asarray(common_w, jnp.float32)[:, None, None]
    positions = jnp.arange(points, dtype=jnp.int32)[:, None]
    is_live = degree[None, :] > 0
    active = ((positions <= degree[None, :]) & is_live).astype(jnp.float32)
    low_sel = ((positions == 0) & is_live).astype(jnp.float32)
    high_sel = ((positions == degree[None, :]) & is_live).astype(jnp.float32)
    return (deriv_sel, weight_sel, inverse_sel, interp_sel, weighted_interp, active, low_sel, high_sel)

def apply_along(matrix, data, axis):
    total = None
    for column in range(matrix.shape[1]):
        piece = lax.index_in_dim(data, column, axis, keepdims=True)
        shape = [1] * data.ndim
        shape[axis] = matrix.shape[0]
        shape[-1] = matrix.shape[-1]
        term = matrix[:, column, :].reshape(shape) * piece
        total = term if total is None else total + term
    return total

def pick_layer(selector, data, axis):
    total = None
    for row in range(selector.shape[0]):
        piece = lax.index_in_dim(data, row, axis, keepdims=False)
        shape = [1] * piece.ndim
        shape[-1] = selector.shape[-1]
        term = selector[row].reshape(shape) * piece
        total = term if total is None else total + term
    return total

def place_layer(selector, layer, axis):
    expanded = jnp.expand_dims(layer, axis)
    shape = [1] * expanded.ndim
    shape[axis] = selector.shape[0]
    shape[-1] = selector.shape[-1]
    return selector.reshape(shape) * expanded

def element_terms(state_rows, setup):
    deriv_sel, weight_sel, inverse_sel, interp_sel, weighted_interp, active, low_sel, high_sel = setup
    points = PMAX + 1
    slot_count = state_rows.shape[-1]
    node_mask = active[:, None, None, :] * active[None, :, None, :] * active[None, None, :, :]
    field = state_rows.reshape(NV, points, points, points, slot_count) * node_mask[None]
    species = field[:9]
    momentum = field[9:12]
    energy = field[12]
    density = lax.optimization_barrier(jnp.sum(species, axis=0))
    safe_rho = jnp.where(node_mask > 0, density, 1.0)
    velocity = momentum / safe_rho[None]
    pressure = 0.4 * (energy - 0.5 * lax.optimization_barrier(jnp.sum(momentum * velocity, axis=0)))
    sound_speed = jnp.sqrt(1.4 * jnp.where(node_mask > 0, pressure, 1.0) / safe_rho)
    volume = jnp.zeros_like(field)
    face_list = []
    for axis_pos in range(3):
        normal_vel = velocity[axis_pos]
        unit = jnp.eye(3, dtype=jnp.float32)[axis_pos].reshape(3, 1, 1, 1, 1)
        flux_dim = jnp.concatenate([species * normal_vel[None], momentum * normal_vel[None] + pressure[None] * unit, ((energy + pressure) * normal_vel)[None]], axis=0) * node_mask[None]
        speeds = (jnp.abs(normal_vel) + sound_speed) * node_mask
        volume = volume + apply_along(deriv_sel, flux_dim, axis_pos + 1)
        for face_side in range(2):
            selector = low_sel if face_side == 0 else high_sel
            normal_sign = -1.0 if face_side == 0 else 1.0
            u_face = pick_layer(selector, field, axis_pos + 1)
            g_face = normal_sign * pick_layer(selector, flux_dim, axis_pos + 1)
            s_face = pick_layer(selector, speeds, axis_pos)
            face_speed = lax.optimization_barrier(jnp.max(s_face, axis=(0, 1)))
            u_common = apply_along(interp_sel, apply_along(interp_sel, u_face, 1), 2)
            g_common = apply_along(interp_sel, apply_along(interp_sel, g_face, 1), 2)
            face_rows = jnp.concatenate([u_common.reshape(NV, points * points, slot_count), g_common.reshape(NV, points * points, slot_count), jnp.broadcast_to(face_speed[None, None, :], (1, points * points, slot_count))], axis=0)
            face_list.append(face_rows)
    traces = jnp.stack(face_list, axis=1)
    return (field, volume, traces, node_mask)

def finish(field, volume, traces, extended, links, setup, node_mask):
    deriv_sel, weight_sel, inverse_sel, interp_sel, weighted_interp, active, low_sel, high_sel = setup
    points = PMAX + 1
    slot_count = field.shape[-1]
    lift_table = weighted_interp.transpose(1, 0, 2)
    surface = jnp.zeros_like(field)
    for face in range(6):
        axis_pos = face // 2
        selector = low_sel if face % 2 == 0 else high_sel
        own_rows = traces[:, face]
        far_rows = jnp.take(extended[:, face ^ 1], links[face], axis=-1)
        penalty = jnp.maximum(own_rows[2 * NV], far_rows[2 * NV])
        jump_flux = 0.5 * (-far_rows[NV:2 * NV] - own_rows[NV:2 * NV]) - 0.5 * penalty[None] * (far_rows[:NV] - own_rows[:NV])
        jump_flux = jump_flux.reshape(NV, points, points, slot_count)
        inv_face = lax.optimization_barrier(jnp.sum(selector * inverse_sel, axis=0))
        lifted = apply_along(lift_table, apply_along(lift_table, jump_flux, 1), 2)
        lifted = lifted * (inverse_sel[None, :, None, :] * inverse_sel[None, None, :, :] * inv_face[None, None, None, :])
        surface = surface + place_layer(selector, lifted, axis_pos + 1)
    section = (field - step_scale * (volume + surface)) * node_mask[None]
    node_weight = weight_sel[:, None, None, :] * weight_sel[None, :, None, :] * weight_sel[None, None, :, :] / 8.0
    species = section[:9]
    average = lax.optimization_barrier(jnp.sum(species * node_weight[None], axis=(1, 2, 3)))
    lowest = lax.optimization_barrier(jnp.min(jnp.where(node_mask[None] > 0, species, 1e+30), axis=(1, 2, 3)))
    scaling = jnp.minimum(1.0, jnp.maximum(average - positivity_eps, 0.0) / jnp.maximum(average - lowest, floor_gap))
    scaled = (average[:, None, None, None, :] + scaling[:, None, None, None, :] * (species - average[:, None, None, None, :])) * node_mask[None]
    return jnp.concatenate([scaled, section[9:]], axis=0).reshape(NV, NODES, slot_count)

def reference(state_send, order_send, send_count, neighbours):
    devices, peer_count = send_count.shape
    slot_count = order_send.shape[0] // devices
    capacity = slot_count // peer_count
    state_view = state_send.reshape(NV, NODES, devices, slot_count)
    positions = jnp.arange(slot_count, dtype=jnp.int32)
    live_send = (positions % capacity)[None, :] < send_count[:, positions // capacity]
    order_tags = jnp.where(live_send, order_send.reshape(devices, slot_count), 0).astype(jnp.int32)
    link_view = neighbours.reshape(6, devices, slot_count)
    zero = jnp.int32(0)

    def migrate(device):
        group_id = (device // peer_count).astype(jnp.int32)
        local_id = (device % peer_count).astype(jnp.int32)
        block_rows = lax.dynamic_slice(state_view, (zero, zero, group_id * peer_count, local_id * capacity), (NV, NODES, peer_count, capacity)).reshape(NV, NODES, slot_count)
        degree = lax.dynamic_slice(order_tags, (group_id * peer_count, local_id * capacity), (peer_count, capacity)).reshape(slot_count)
        return (block_rows, degree)

    def first_pass(device):
        block_rows, degree = migrate(device)
        return element_terms(block_rows, selections(degree))[2]
    device_ids = jnp.arange(devices, dtype=jnp.int32)
    all_traces = lax.map(first_pass, device_ids)

    def second_pass(device):
        block_rows, degree = migrate(device)
        setup = selections(degree)
        field, volume, traces, node_mask = element_terms(block_rows, setup)
        before = all_traces[jnp.maximum(device - 1, 0)][..., slot_count - BAND:] * (device > 0).astype(jnp.float32)
        after = all_traces[jnp.minimum(device + 1, devices - 1)][..., :BAND] * (device < devices - 1).astype(jnp.float32)
        extended = jnp.concatenate([before, traces, after], axis=-1)
        links = lax.dynamic_index_in_dim(link_view, device, axis=1, keepdims=False)
        return finish(field, volume, traces, extended, links, setup, node_mask)
    result = lax.map(second_pass, device_ids)
    return result.transpose(1, 2, 0, 3).reshape(NV, NODES, devices * slot_count)
```

```python
import jax
import jax.numpy as jnp
import numpy as np
from jax import lax
from jax.experimental import pallas as pl
from jax.experimental.pallas import tpu as pltpu
from jax.sharding import PartitionSpec as P

NV = 13
PMAX = 5
PTS = PMAX + 1
NODES = 216
FACE = 36
BAND = 16
SLOTS = 128
ROWS = 22
PITCH = 24
FEATS = ROWS * 128
HALO = 216

step_scale = 0.02
positivity_eps = 0.001
floor_gap = 0.05

AXES = ("gx", "gy", "gz")
GROUP = ("gy", "gz")
D0, M1, M2, W0, ACT, OWN_ROWS = 0, 40, 80, 120, 128, 136


def lagrange_coeffs(node_pos, column):
    coeffs = [1.0]
    denom = 1.0
    for other in range(len(node_pos)):
        if other == column:
            continue
        shifted = [0.0] * (len(coeffs) + 1)
        for power in range(len(coeffs)):
            shifted[power + 1] += coeffs[power]
            shifted[power] -= float(node_pos[other]) * coeffs[power]
        coeffs = shifted
        denom = denom * (float(node_pos[column]) - float(node_pos[other]))
    return [value / denom for value in coeffs]


def poly_value(coeffs, point):
    total = 0.0
    for power in range(len(coeffs)):
        total += coeffs[power] * point**power
    return total


def poly_slope(coeffs, point):
    total = 0.0
    for power in range(1, len(coeffs)):
        total += power * coeffs[power] * point ** (power - 1)
    return total


def poly_integral(coeffs):
    total = 0.0
    for power in range(len(coeffs)):
        total += coeffs[power] * (1.0 - (-1.0) ** (power + 1)) / (power + 1)
    return total


def basis_tables():
    points = PMAX + 1
    common = np.linspace(-1.0, 1.0, points)
    derivs = np.zeros((PMAX, points, points))
    weights = np.zeros((PMAX, points))
    inverse = np.zeros((PMAX, points))
    interp = np.zeros((PMAX, points, points))
    for degree in range(1, PMAX + 1):
        node_pos = np.linspace(-1.0, 1.0, degree + 1)
        for column in range(degree + 1):
            coeffs = lagrange_coeffs(node_pos, column)
            weights[degree - 1, column] = poly_integral(coeffs)
            for row in range(points):
                interp[degree - 1, row, column] = poly_value(coeffs, float(common[row]))
            for row in range(degree + 1):
                derivs[degree - 1, row, column] = poly_slope(coeffs, float(node_pos[row]))
        inverse[degree - 1, : degree + 1] = 1.0 / weights[degree - 1, : degree + 1]
    return (derivs, weights, inverse, interp, weights[PMAX - 1].copy())


def shell_order():
    nodes = [(a, b, c) for a in range(PTS) for b in range(PTS) for c in range(PTS)]
    ranked = sorted(range(NODES), key=lambda n: (max(1, *nodes[n]), n))
    rank = [0] * NODES
    for r, n in enumerate(ranked):
        rank[n] = r
    return rank, [max(1, *abc) for abc in nodes]


RANK, LEVEL = shell_order()


def element_tables():
    derivs, weights, inverse, interp, common = basis_tables()
    own = np.zeros((OWN_ROWS, 128))
    far = np.zeros((80, 128))
    for p in range(1, PMAX + 1):
        deriv, weight, inv, value = (derivs[p - 1], weights[p - 1], inverse[p - 1], interp[p - 1])
        own[D0 : D0 + 36, p] = -step_scale * deriv.reshape(36)
        lift = inv[:, None] * value.T * common[None, :]
        both = lift @ value
        own[M1 : M1 + 36, p] = both.reshape(36)
        own[M2 : M2 + 36, p] = step_scale * inv[0] * both.reshape(36)
        own[W0 : W0 + 6, p] = 0.5 * weight
        own[ACT : ACT + p + 1, p] = 1.0
        for r in range(1, PMAX + 1):
            both = lift @ interp[r - 1]
            column = (p - 1) * 5 + (r - 1)
            far[0:36, column] = both.reshape(36)
            far[40:76, column] = -step_scale * inv[0] * both.reshape(36)
    return jnp.asarray(own, jnp.float32), jnp.asarray(far, jnp.float32)


def iota(shape, axis):
    return lax.broadcasted_iota(jnp.int32, shape, axis)


def row8(ref, row):
    return jnp.broadcast_to(ref[pl.ds(row, 1), :], (8, SLOTS))


def node_of(axis, layer, b, c):
    if axis == 0:
        return layer * 36 + b * 6 + c
    if axis == 1:
        return b * 36 + layer * 6 + c
    return b * 36 + c * 6 + layer


def block(ref, index, unit=8, offset=0):
    if isinstance(index, int):
        start = index * unit + offset
    else:
        start = pl.multiple_of(index * unit + offset, 8)
    return ref.at[pl.ds(start, 8), :]


def pack_body(peers, state, order, count, out, feats):
    capacity = SLOTS // peers
    spread = (iota((peers, SLOTS), 1) // capacity == iota((peers, SLOTS), 0)).astype(jnp.float32)
    counts = jnp.broadcast_to(count[...].astype(jnp.float32), (8, peers))
    per_slot = jnp.dot(counts, spread, preferred_element_type=jnp.float32)
    place = (iota((8, SLOTS), 1) % capacity).astype(jnp.float32)
    orders = jnp.broadcast_to(order[...].astype(jnp.float32), (8, SLOTS))
    tag = jnp.where(place < per_slot, orders, 0.0)
    for n in range(NODES):
        feats[pl.ds(RANK[n] * NV, NV), :] = state[pl.ds(n, NV, stride=NODES), :]
    feats[pl.ds(NODES * NV, 8), :] = tag
    for k in range(ROWS):
        out[pl.ds(k, SLOTS, stride=PITCH), :] = feats[pl.ds(k * 128, 128), :].T


def pack(state, order, count):
    peers = count.shape[-1]
    return pl.pallas_call(
        lambda *refs: pack_body(peers, *refs),
        out_shape=jax.ShapeDtypeStruct((SLOTS * PITCH, 128), jnp.float32),
        scratch_shapes=[pltpu.VMEM((FEATS, SLOTS), jnp.float32)],
        name="pack",
    )(state, order, count)


def prep_body(recv, own_table, a_ref, b_ref, high, up, down, tab, order, feats):
    for k in range(ROWS):
        feats[pl.ds(k * 128, 128), :] = recv[pl.ds(k, SLOTS, stride=PITCH), :].T
    ob = row8(feats, NODES * NV)
    order[...] = ob
    pick = (iota((128, SLOTS), 0).astype(jnp.float32) == ob[0:1, :]).astype(jnp.float32)
    tab[...] = jnp.dot(
        own_table[...], pick, precision=lax.Precision.HIGHEST, preferred_element_type=jnp.float32
    )
    live = [None] + [ob >= float(m) for m in range(1, PMAX + 1)]
    for n in range(NODES):
        act = live[LEVEL[n]]
        first = RANK[n] * NV
        a_ref[pl.ds(n * 8, 8), :] = jnp.where(act, feats[pl.ds(first, 8), :], 0.0)
        second = jnp.where(act, feats[pl.ds(first + 8, 8), :], 0.0)
        for axis in range(3):
            b_ref[pl.ds((axis * NODES + n) * 8, 8), :] = second
    lane_row = iota((8, SLOTS), 0)

    def primitives(g, carry):
        n = g * 8 + lane_row
        top = jnp.maximum(jnp.maximum(n // 36, (n // 6) % 6), jnp.maximum(n % 6, 1))
        act = ob >= top.astype(jnp.float32)
        base = g * 64
        species = [a_ref[pl.ds(base + v, 8, stride=8), :] for v in range(8)]
        species.append(b_ref[pl.ds(base, 8, stride=8), :])
        momentum = [b_ref[pl.ds(base + 1 + i, 8, stride=8), :] for i in range(3)]
        energy = b_ref[pl.ds(base + 4, 8, stride=8), :]
        rho = species[0]
        for value in species[1:]:
            rho = rho + value
        inv = 1.0 / jnp.where(act, rho, 1.0)
        velocity = [value * inv for value in momentum]
        kinetic = momentum[0] * velocity[0] + momentum[1] * velocity[1] + momentum[2] * velocity[2]
        pressure = 0.4 * (energy - 0.5 * kinetic)
        sound = jnp.sqrt(1.4 * jnp.where(act, pressure, 1.0) * inv)
        for axis in range(3):
            start = axis * NODES * 8 + base
            b_ref[pl.ds(start + 5, 8, stride=8), :] = pressure
            b_ref[pl.ds(start + 6, 8, stride=8), :] = velocity[axis]
            b_ref[pl.ds(start + 7, 8, stride=8), :] = jnp.where(
                act, jnp.abs(velocity[axis]) + sound, 0.0
            )
        return carry

    lax.fori_loop(0, NODES // 8, primitives, 0)
    is_top = [None] + [ob == float(m) for m in range(1, PMAX + 1)]
    lane = iota((8, SLOTS), 1)
    group = lane // BAND
    up_now = down_now = None
    for axis in range(3):
        for q in range(FACE):
            b, c = divmod(q, 6)
            for part in range(2):
                ref = a_ref if part == 0 else b_ref
                shift = 0 if part == 0 else axis * NODES

                def read(layer):
                    return ref[pl.ds((shift + node_of(axis, layer, b, c)) * 8, 8), :]

                top = read(1)
                for m in range(2, PMAX + 1):
                    top = jnp.where(is_top[m], read(m), top)
                index = (axis * FACE + q) * 2 + part
                high[pl.ds(index * 8, 8), :] = top
                word, k = divmod(index, 8)
                moved_up = pltpu.roll(top, (16 * k - (SLOTS - BAND)) % SLOTS, 1)
                low = read(0)
                moved_down = pltpu.roll(low, 16 * k, 1) if k else low
                up_now = moved_up if k == 0 else jnp.where(group == k, moved_up, up_now)
                down_now = moved_down if k == 0 else jnp.where(group == k, moved_down, down_now)
                if k == 7:
                    up[pl.ds(word * 8, 8), :] = up_now
                    down[pl.ds(word * 8, 8), :] = down_now
    up[pl.ds(HALO, 8), :] = pltpu.roll(ob, BAND, 1)
    down[pl.ds(HALO, 8), :] = ob


def prep(recv, own_table):
    shape = lambda rows: jax.ShapeDtypeStruct((rows, SLOTS), jnp.float32)
    return pl.pallas_call(
        prep_body,
        out_shape=(
            shape(NODES * 8),
            shape(3 * NODES * 8),
            shape(3 * FACE * 16),
            shape(HALO + 8),
            shape(HALO + 8),
            shape(OWN_ROWS),
            shape(8),
        ),
        scratch_shapes=[pltpu.VMEM((FEATS, SLOTS), jnp.float32)],
        name="prep",
    )(recv, own_table)


def flux_rows(axis, scale):
    rows = iota((8, SLOTS), 0)
    return (
        jnp.where(rows == 1 + axis, scale, 0.0).astype(jnp.float32),
        jnp.where(rows == 4, scale, 0.0).astype(jnp.float32),
    )


def volume_body(a_ref, b_ref, tab, acc):
    for axis in range(3):
        normal_row, energy_row = flux_rows(axis, 1.0)
        stride = (36, 6, 1)[axis]

        def pencil(t, carry):
            base = (t, (t // 6) * 36 + t % 6, t * 6)[axis]
            flux_a, flux_b = [], []
            for j in range(6):
                n = base + j * stride
                where = pl.multiple_of((axis * NODES + n) * 8, 8)
                speed = row8(b_ref, where + 6)
                pressure = row8(b_ref, where + 5)
                flux_a.append(block(a_ref, n)[...] * speed)
                flux_b.append(
                    b_ref[pl.ds(where, 8), :] * speed
                    + pressure * (normal_row + energy_row * speed)
                )
            for i in range(6):
                n = base + i * stride
                if axis == 0:
                    sum_a = block(a_ref, n)[...]
                    sum_b = block(b_ref, n)[...]
                else:
                    sum_a = block(acc, n, 16)[...]
                    sum_b = block(acc, n, 16, 8)[...]
                for j in range(6):
                    factor = row8(tab, D0 + i * 6 + j)
                    sum_a = sum_a + factor * flux_a[j]
                    sum_b = sum_b + factor * flux_b[j]
                block(acc, n, 16)[...] = sum_a
                block(acc, n, 16, 8)[...] = sum_b
            return carry

        lax.fori_loop(0, FACE, pencil, 0)


def volume(a, b, tab):
    return pl.pallas_call(
        volume_body,
        out_shape=jax.ShapeDtypeStruct((NODES * 16, SLOTS), jnp.float32),
        name="volume",
    )(a, b, tab)


def gather_lanes(value, index):
    return jnp.take_along_axis(value, index, axis=1)


def finish_body(
    a_ref, b_ref, high, acc_in, tab, order, links, before, after, far_table,
    out, acc, far, own_mid, far_mid, pair,
):
    acc[...] = acc_in[...]
    ob = order[...]
    for face in range(6):
        axis, side = divmod(face, 2)
        sign = 0.5 if side else -0.5
        halo = after if side else before
        link = jnp.broadcast_to(links[pl.ds(face, 1), :], (8, SLOTS))
        outside = link >= BAND + SLOTS if side else link < BAND
        halo_lane = jnp.where(outside, link - (BAND + SLOTS if side else 0), 0)
        own_lane = jnp.clip(link - BAND, 0, SLOTS - 1)
        far_order = jnp.where(
            outside,
            gather_lanes(halo[pl.ds(HALO, 8), :], halo_lane),
            gather_lanes(ob, own_lane),
        )
        column = jnp.where(ob > 0.0, (ob - 1.0) * 5.0 + far_order - 1.0, -1.0)
        pick = (iota((128, SLOTS), 0).astype(jnp.float32) == column[0:1, :]).astype(jnp.float32)
        pair[...] = jnp.dot(
            far_table[...],
            pick,
            precision=lax.Precision.HIGHEST,
            preferred_element_type=jnp.float32,
        )

        def low_block(part, q):
            b, c = divmod(q, 6)
            n = node_of(axis, 0, b, c)
            if part == 0:
                return a_ref[pl.ds(n * 8, 8), :]
            return b_ref[pl.ds((axis * NODES + n) * 8, 8), :]

        def high_block(part, q):
            return high[pl.ds(((axis * FACE + q) * 2 + part) * 8, 8), :]

        inner, outer = (high_block, low_block) if side else (low_block, high_block)
        fastest = None
        for q in range(FACE):
            for part in range(2):
                word, k = divmod((axis * FACE + q) * 2 + part, 8)
                here = gather_lanes(outer(part, q), own_lane)
                there = gather_lanes(halo[pl.ds(word * 8, 8), :], halo_lane + 16 * k)
                value = jnp.where(outside, there, here)
                far[pl.ds((q * 2 + part) * 8, 8), :] = value
                if part == 1:
                    value = jnp.maximum(value, inner(1, q))
                    fastest = value if fastest is None else jnp.maximum(fastest, value)
        penalty = 0.5 * jnp.broadcast_to(fastest[7:8, :], (8, SLOTS))
        normal_row, energy_row = flux_rows(axis, sign)

        def weighted(block_a, ref_b, start):
            start = pl.multiple_of(start, 8)
            speed = row8(ref_b, start + 6)
            pressure = row8(ref_b, start + 5)
            mix = sign * speed - penalty
            return (
                block_a * mix,
                ref_b[pl.ds(start, 8), :] * mix + pressure * (normal_row + energy_row * speed),
            )

        def first(k, carry):
            for ours in (True, False):
                points = []
                for j in range(6):
                    if not ours:
                        start = (j * 6 + k) * 16
                        points.append(weighted(block(far, j * 6 + k, 16)[...], far, start + 8))
                    elif side:
                        index = axis * FACE + j * 6 + k
                        points.append(weighted(block(high, index, 16)[...], high, index * 16 + 8))
                    else:
                        n = node_of(axis, 0, j, k)
                        points.append(weighted(block(a_ref, n)[...], b_ref, (axis * NODES + n) * 8))
                table, offset, mid = (tab, M1, own_mid) if ours else (pair, 0, far_mid)
                for b in range(6):
                    for part in range(2):
                        total = None
                        for j in range(6):
                            term = row8(table, offset + b * 6 + j) * points[j][part]
                            total = term if total is None else total + term
                        block(mid, b * 6 + k, 16, 8 * part)[...] = total
            return carry

        def second(b, carry):
            for c in range(6):
                for part in range(2):
                    total = None
                    for k in range(6):
                        term = row8(tab, M2 + c * 6 + k) * block(own_mid, b * 6 + k, 16, 8 * part)[...]
                        term = term + row8(pair, 40 + c * 6 + k) * block(far_mid, b * 6 + k, 16, 8 * part)[...]
                        total = term if total is None else total + term
                    if side == 0:
                        place = block(acc, node_of(axis, 0, b, c), 16, 8 * part)
                        place[...] = place[...] + total
                    else:
                        for layer in range(1, 6):
                            place = block(acc, node_of(axis, layer, b, c), 16, 8 * part)
                            place[...] = place[...] + jnp.where(ob == float(layer), total, 0.0)
            return carry

        lax.fori_loop(0, 6, first, 0)
        lax.fori_loop(0, 6, second, 0)

    zero = jnp.zeros((8, SLOTS), jnp.float32)
    large = jnp.full((8, SLOTS), 1e30, jnp.float32)

    def reduce(t, carry):
        mean_a, mean_b, low_a, low_b = carry
        weight = row8(tab, W0 + t // 6) * row8(tab, W0 + t % 6)
        active = row8(tab, ACT + t // 6) * row8(tab, ACT + t % 6)
        for c in range(6):
            value_a = block(acc, t * 6 + c, 16)[...]
            value_b = block(acc, t * 6 + c, 16, 8)[...]
            here = weight * row8(tab, W0 + c)
            mask = active * row8(tab, ACT + c) > 0.0
            mean_a = mean_a + value_a * here
            mean_b = mean_b + value_b * here
            low_a = jnp.minimum(low_a, jnp.where(mask, value_a, 1e30))
            low_b = jnp.minimum(low_b, jnp.where(mask, value_b, 1e30))
        return mean_a, mean_b, low_a, low_b

    mean_a, mean_b, low_a, low_b = lax.fori_loop(0, FACE, reduce, (zero, zero, large, large))

    def limiter(mean, low):
        return jnp.minimum(
            1.0, jnp.maximum(mean - positivity_eps, 0.0) / jnp.maximum(mean - low, floor_gap)
        )

    scale_a, scale_b = limiter(mean_a, low_a), limiter(mean_b, low_b)
    is_species = iota((8, SLOTS), 0) == 0

    def write(t, carry):
        active = row8(tab, ACT + t // 6) * row8(tab, ACT + t % 6)
        for c in range(6):
            n = t * 6 + c
            value_a = block(acc, n, 16)[...]
            value_b = block(acc, n, 16, 8)[...]
            mask = active * row8(tab, ACT + c) > 0.0
            value_a = jnp.where(mask, mean_a + scale_a * (value_a - mean_a), 0.0)
            scaled = jnp.where(is_species, mean_b + scale_b * (value_b - mean_b), value_b)
            value_b = jnp.where(mask, scaled, 0.0)
            out[pl.ds(n, 8, stride=NODES), :] = value_a
            out[pl.ds(8 * NODES + n, 5, stride=NODES), :] = value_b[0:5, :]
        return carry

    lax.fori_loop(0, FACE, write, 0)


def finish(a, b, high, acc, tab, order, links, before, after, far_table):
    vmem = lambda rows: pltpu.VMEM((rows, SLOTS), jnp.float32)
    return pl.pallas_call(
        finish_body,
        out_shape=jax.ShapeDtypeStruct((NV * NODES, SLOTS), jnp.float32),
        scratch_shapes=[vmem(NODES * 16), vmem(FACE * 16), vmem(FACE * 16), vmem(FACE * 16), vmem(80)],
        name="finish",
    )(a, b, high, acc, tab, order, links, before, after, far_table)


def local(state_send, order_send, send_count, neighbours):
    peers = lax.axis_size(GROUP)
    own_table, far_table = element_tables()
    packed = pack(
        state_send.reshape(NV * NODES, SLOTS), order_send.reshape(1, SLOTS), send_count
    )
    blocks = packed.reshape(peers, SLOTS // peers * PITCH, 128)
    moved = lax.all_to_all(blocks, GROUP, split_axis=0, concat_axis=0, tiled=True)
    a, b, high, up, down, tab, order = prep(moved.reshape(SLOTS * PITCH, 128), own_table)
    devices = lax.axis_size(AXES)
    forward = [(i, i + 1) for i in range(devices - 1)]
    before = lax.ppermute(up, AXES, forward)
    after = lax.ppermute(down, AXES, [(j, i) for i, j in forward])
    acc = volume(a, b, tab)
    result = finish(a, b, high, acc, tab, order, neighbours, before, after, far_table)
    return result.reshape(NV, NODES, SLOTS)


def solution(mesh):
    placed = (
        P(None, None, AXES),
        P(AXES),
        P(AXES, None),
        P(None, AXES),
    )
    return jax.shard_map(
        local,
        mesh=mesh,
        in_specs=placed,
        out_specs=P(None, None, AXES),
        check_vma=False,
    )
```

```python
import jax
import jax.numpy as jnp
import numpy as np
from jax import lax
from jax.experimental import pallas as pl
from jax.experimental.pallas import tpu as pltpu
from jax.sharding import Mesh, PartitionSpec as P


NV = 13
PMAX = 5
PTS = PMAX + 1
NODES = 216
FACE = 36
BAND = 16
SLOTS = 128
ROWS = 22
PITCH = 24
FEATS = ROWS * 128
HALO = 216
HALF = SLOTS // 2
HEAD = 8
ROOM = 584
FLAG = 22

step_scale = 0.02
positivity_eps = 0.001
floor_gap = 0.05

AXES = ("gx", "y", "zh", "gz")
GROUP = ("y", "zh", "gz")
SIDE = ("y", "gz")
D0, M1, M2, W0, ACT, OWN_ROWS = 0, 40, 80, 120, 128, 136


def lagrange_coeffs(node_pos, column):
    coeffs = [1.0]
    denom = 1.0
    for other in range(len(node_pos)):
        if other == column:
            continue
        shifted = [0.0] * (len(coeffs) + 1)
        for power in range(len(coeffs)):
            shifted[power + 1] += coeffs[power]
            shifted[power] -= float(node_pos[other]) * coeffs[power]
        coeffs = shifted
        denom = denom * (float(node_pos[column]) - float(node_pos[other]))
    return [value / denom for value in coeffs]


def poly_value(coeffs, point):
    total = 0.0
    for power in range(len(coeffs)):
        total += coeffs[power] * point**power
    return total


def poly_slope(coeffs, point):
    total = 0.0
    for power in range(1, len(coeffs)):
        total += power * coeffs[power] * point ** (power - 1)
    return total


def poly_integral(coeffs):
    total = 0.0
    for power in range(len(coeffs)):
        total += coeffs[power] * (1.0 - (-1.0) ** (power + 1)) / (power + 1)
    return total


def basis_tables():
    points = PMAX + 1
    common = np.linspace(-1.0, 1.0, points)
    derivs = np.zeros((PMAX, points, points))
    weights = np.zeros((PMAX, points))
    inverse = np.zeros((PMAX, points))
    interp = np.zeros((PMAX, points, points))
    for degree in range(1, PMAX + 1):
        node_pos = np.linspace(-1.0, 1.0, degree + 1)
        for column in range(degree + 1):
            coeffs = lagrange_coeffs(node_pos, column)
            weights[degree - 1, column] = poly_integral(coeffs)
            for row in range(points):
                interp[degree - 1, row, column] = poly_value(coeffs, float(common[row]))
            for row in range(degree + 1):
                derivs[degree - 1, row, column] = poly_slope(coeffs, float(node_pos[row]))
        inverse[degree - 1, : degree + 1] = 1.0 / weights[degree - 1, : degree + 1]
    return (derivs, weights, inverse, interp, weights[PMAX - 1].copy())


def shell_order():
    nodes = [(a, b, c) for a in range(PTS) for b in range(PTS) for c in range(PTS)]
    ranked = sorted(range(NODES), key=lambda n: (max(1, *nodes[n]), n))
    rank = [0] * NODES
    for r, n in enumerate(ranked):
        rank[n] = r
    return rank, [max(1, *abc) for abc in nodes]


RANK, LEVEL = shell_order()


def element_tables():
    derivs, weights, inverse, interp, common = basis_tables()
    own = np.zeros((OWN_ROWS, 128))
    far = np.zeros((80, 128))
    for p in range(1, PMAX + 1):
        deriv, weight, inv, value = (derivs[p - 1], weights[p - 1], inverse[p - 1], interp[p - 1])
        own[D0 : D0 + 36, p] = -step_scale * deriv.reshape(36)
        lift = inv[:, None] * value.T * common[None, :]
        both = lift @ value
        own[M1 : M1 + 36, p] = both.reshape(36)
        own[M2 : M2 + 36, p] = step_scale * inv[0] * both.reshape(36)
        own[W0 : W0 + 6, p] = 0.5 * weight
        own[ACT : ACT + p + 1, p] = 1.0
        for r in range(1, PMAX + 1):
            both = lift @ interp[r - 1]
            column = (p - 1) * 5 + (r - 1)
            far[0:36, column] = both.reshape(36)
            far[40:76, column] = -step_scale * inv[0] * both.reshape(36)
    return jnp.asarray(own, jnp.float32), jnp.asarray(far, jnp.float32)


def iota(shape, axis):
    return lax.broadcasted_iota(jnp.int32, shape, axis)


def row8(ref, row):
    return jnp.broadcast_to(ref[pl.ds(row, 1), :], (8, SLOTS))


def node_of(axis, layer, b, c):
    if axis == 0:
        return layer * 36 + b * 6 + c
    if axis == 1:
        return b * 36 + layer * 6 + c
    return b * 36 + c * 6 + layer


def block(ref, index, unit=8, offset=0):
    if isinstance(index, int):
        start = index * unit + offset
    else:
        start = pl.multiple_of(index * unit + offset, 8)
    return ref.at[pl.ds(start, 8), :]


def slot_tags(peers, order, count):
    capacity = SLOTS // peers
    spread = (iota((peers, SLOTS), 1) // capacity == iota((peers, SLOTS), 0)).astype(jnp.float32)
    counts = jnp.broadcast_to(count[...].astype(jnp.float32), (8, peers))
    per_slot = jnp.dot(counts, spread, preferred_element_type=jnp.float32)
    place = (iota((8, SLOTS), 1) % capacity).astype(jnp.float32)
    orders = jnp.broadcast_to(order[...].astype(jnp.float32), (8, SLOTS))
    return jnp.where(place < per_slot, orders, 0.0)


def transpose_elements(state, tag, out, feats):
    for n in range(NODES):
        feats[pl.ds(RANK[n] * NV, NV), :] = state[pl.ds(n, NV, stride=NODES), :]
    feats[pl.ds(NODES * NV, 8), :] = tag
    for k in range(ROWS):
        out[pl.ds(k, SLOTS, stride=PITCH), :] = feats[pl.ds(k * 128, 128), :].T


def pack_all_body(peers, state, order, count, out, feats):
    transpose_elements(state, slot_tags(peers, order, count), out, feats)


def pack_all(state, order, count):
    peers = count.shape[-1]
    return pl.pallas_call(
        lambda *refs: pack_all_body(peers, *refs),
        out_shape=jax.ShapeDtypeStruct((SLOTS * PITCH, 128), jnp.float32),
        scratch_shapes=[pltpu.VMEM((FEATS, SLOTS), jnp.float32)],
        name="pack_all",
    )(state, order, count)


def rows_of(order):
    rows = jnp.where(order == 5, 22, jnp.where(order == 4, 13, 7))
    return jnp.where(order == 3, rows, jnp.where(order == 2, 3, jnp.where(order == 1, 1, jnp.where(order == 0, 0, rows))))


def pack_body(peers, chunk, side, order_s, count_s, state, order, count, own, away, feats, rows, room):
    capacity = SLOTS // peers
    tag = slot_tags(peers, order, count)
    transpose_elements(state, tag, rows, feats)
    zh = side[0]

    def send(e, total):
        slot = (e // chunk) * (2 * chunk) + (1 - zh) * chunk + e % chunk
        alive = slot % capacity < count_s[slot // capacity]
        used = jnp.where(alive, rows_of(order_s[slot]), 0)
        offset = jnp.minimum(total, ROOM)
        room[pl.ds(offset, PITCH), :] = rows[pl.ds(pl.multiple_of(slot * PITCH, 8), PITCH), :]
        return total + used

    total = lax.fori_loop(0, HALF, send, jnp.int32(0))
    away[pl.ds(0, HEAD), :] = tag
    away[pl.ds(HEAD, ROOM), :] = room[pl.ds(0, ROOM), :]
    flag = jnp.full((1, 128), jnp.where(total > ROOM, 1.0, 0.0), jnp.float32)
    for y in range(HALF // chunk):
        start = pl.multiple_of((2 * chunk * y + chunk * zh) * PITCH, 8)
        own[pl.ds(y * chunk * PITCH, chunk * PITCH), :] = rows[pl.ds(start, chunk * PITCH), :]
    for e in range(0, HALF, capacity):
        own[pl.ds(e * PITCH + FLAG, 1), :] = flag


def pack(state, order, count, side, chunk):
    peers = count.shape[-1]
    vmem = lambda rows: pltpu.VMEM((rows, 128), jnp.float32)
    whole = pl.BlockSpec(memory_space=pltpu.VMEM)
    scalar = pl.BlockSpec(memory_space=pltpu.SMEM)
    return pl.pallas_call(
        lambda *refs: pack_body(peers, chunk, *refs),
        in_specs=[scalar, scalar, scalar, whole, whole, whole],
        out_shape=(
            jax.ShapeDtypeStruct((HALF * PITCH, 128), jnp.float32),
            jax.ShapeDtypeStruct((HEAD + ROOM, 128), jnp.float32),
        ),
        scratch_shapes=[vmem(FEATS), vmem(SLOTS * PITCH), vmem(ROOM + PITCH)],
        name="pack",
    )(side, order, count.reshape(peers), state, order.reshape(1, SLOTS), count)


def unpack_body(capacity, chunk, side, tags, came, out, room):
    zh = side[0]
    room[pl.ds(0, ROOM), :] = came[pl.ds(HEAD, ROOM), :]
    lane = iota((1, 128), 1)

    def take(e, total):
        slot = (e // chunk) * (2 * chunk) + zh * chunk + e % chunk
        order = tags[0, slot]
        offset = jnp.minimum(total, ROOM)
        start = pl.multiple_of(e * PITCH, 8)
        out[pl.ds(start, PITCH), :] = room[pl.ds(offset, PITCH), :]
        last = out[pl.ds(start + ROWS - 1, 1), :]
        out[pl.ds(start + ROWS - 1, 1), :] = jnp.where(lane >= 120, order, last)
        return total + rows_of(order)

    total = lax.fori_loop(0, HALF, take, jnp.int32(0))
    flag = jnp.full((1, 128), jnp.where(total > ROOM, 1.0, 0.0), jnp.float32)
    for e in range(0, HALF, capacity):
        out[pl.ds(e * PITCH + FLAG, 1), :] = flag


def unpack(came, side, capacity, chunk):
    return pl.pallas_call(
        lambda *refs: unpack_body(capacity, chunk, *refs),
        grid=(1,),
        in_specs=[
            pl.BlockSpec(memory_space=pltpu.SMEM),
            pl.BlockSpec((HEAD, 128), lambda i: (0, 0), memory_space=pltpu.SMEM),
            pl.BlockSpec((HEAD + ROOM, 128), lambda i: (0, 0)),
        ],
        out_specs=pl.BlockSpec((HALF * PITCH, 128), lambda i: (0, 0)),
        out_shape=jax.ShapeDtypeStruct((HALF * PITCH, 128), jnp.float32),
        scratch_shapes=[pltpu.VMEM((ROOM + PITCH, 128), jnp.float32)],
        name="unpack",
    )(side, came, came)


def prep_body(chunk, side, near, away, own_table, a_ref, b_ref, high, up, down, tab, order, feats, recv):
    zh = side[0]
    for y in range(HALF // chunk):
        size = chunk * PITCH
        for source, half in ((near, zh), (away, 1 - zh)):
            start = pl.multiple_of((2 * chunk * y + chunk * half) * PITCH, 8)
            recv[pl.ds(start, size), :] = source[pl.ds(y * size, size), :]
    for k in range(ROWS):
        feats[pl.ds(k * 128, 128), :] = recv[pl.ds(k, SLOTS, stride=PITCH), :].T
    ob = row8(feats, NODES * NV)
    order[...] = ob
    pick = (iota((128, SLOTS), 0).astype(jnp.float32) == ob[0:1, :]).astype(jnp.float32)
    tab[...] = jnp.dot(
        own_table[...], pick, precision=lax.Precision.HIGHEST, preferred_element_type=jnp.float32
    )
    live = [None] + [ob >= float(m) for m in range(1, PMAX + 1)]
    for n in range(NODES):
        act = live[LEVEL[n]]
        first = RANK[n] * NV
        a_ref[pl.ds(n * 8, 8), :] = jnp.where(act, feats[pl.ds(first, 8), :], 0.0)
        second = jnp.where(act, feats[pl.ds(first + 8, 8), :], 0.0)
        for axis in range(3):
            b_ref[pl.ds((axis * NODES + n) * 8, 8), :] = second
    lane_row = iota((8, SLOTS), 0)

    def primitives(g, carry):
        n = g * 8 + lane_row
        top = jnp.maximum(jnp.maximum(n // 36, (n // 6) % 6), jnp.maximum(n % 6, 1))
        act = ob >= top.astype(jnp.float32)
        base = g * 64
        species = [a_ref[pl.ds(base + v, 8, stride=8), :] for v in range(8)]
        species.append(b_ref[pl.ds(base, 8, stride=8), :])
        momentum = [b_ref[pl.ds(base + 1 + i, 8, stride=8), :] for i in range(3)]
        energy = b_ref[pl.ds(base + 4, 8, stride=8), :]
        rho = species[0]
        for value in species[1:]:
            rho = rho + value
        inv = 1.0 / jnp.where(act, rho, 1.0)
        velocity = [value * inv for value in momentum]
        kinetic = momentum[0] * velocity[0] + momentum[1] * velocity[1] + momentum[2] * velocity[2]
        pressure = 0.4 * (energy - 0.5 * kinetic)
        sound = jnp.sqrt(1.4 * jnp.where(act, pressure, 1.0) * inv)
        for axis in range(3):
            start = axis * NODES * 8 + base
            b_ref[pl.ds(start + 5, 8, stride=8), :] = pressure
            b_ref[pl.ds(start + 6, 8, stride=8), :] = velocity[axis]
            b_ref[pl.ds(start + 7, 8, stride=8), :] = jnp.where(
                act, jnp.abs(velocity[axis]) + sound, 0.0
            )
        return carry

    lax.fori_loop(0, NODES // 8, primitives, 0)
    is_top = [None] + [ob == float(m) for m in range(1, PMAX + 1)]
    lane = iota((8, SLOTS), 1)
    group = lane // BAND
    up_now = down_now = None
    for axis in range(3):
        for q in range(FACE):
            b, c = divmod(q, 6)
            for part in range(2):
                ref = a_ref if part == 0 else b_ref
                shift = 0 if part == 0 else axis * NODES

                def read(layer):
                    return ref[pl.ds((shift + node_of(axis, layer, b, c)) * 8, 8), :]

                top = read(1)
                for m in range(2, PMAX + 1):
                    top = jnp.where(is_top[m], read(m), top)
                index = (axis * FACE + q) * 2 + part
                high[pl.ds(index * 8, 8), :] = top
                word, k = divmod(index, 8)
                moved_up = pltpu.roll(top, (16 * k - (SLOTS - BAND)) % SLOTS, 1)
                low = read(0)
                moved_down = pltpu.roll(low, 16 * k, 1) if k else low
                up_now = moved_up if k == 0 else jnp.where(group == k, moved_up, up_now)
                down_now = moved_down if k == 0 else jnp.where(group == k, moved_down, down_now)
                if k == 7:
                    up[pl.ds(word * 8, 8), :] = up_now
                    down[pl.ds(word * 8, 8), :] = down_now
    up[pl.ds(HALO, 8), :] = pltpu.roll(ob, BAND, 1)
    down[pl.ds(HALO, 8), :] = ob


def prep(near, away, own_table, side, chunk):
    whole = pl.BlockSpec(memory_space=pltpu.VMEM)
    shape = lambda rows: jax.ShapeDtypeStruct((rows, SLOTS), jnp.float32)
    return pl.pallas_call(
        lambda *refs: prep_body(chunk, *refs),
        in_specs=[pl.BlockSpec(memory_space=pltpu.SMEM), whole, whole, whole],
        out_shape=(
            shape(NODES * 8),
            shape(3 * NODES * 8),
            shape(3 * FACE * 16),
            shape(HALO + 8),
            shape(HALO + 8),
            shape(OWN_ROWS),
            shape(8),
        ),
        scratch_shapes=[
            pltpu.VMEM((FEATS, SLOTS), jnp.float32),
            pltpu.VMEM((SLOTS * PITCH, 128), jnp.float32),
        ],
        name="prep",
    )(side, near, away, own_table)


def flux_rows(axis, scale):
    rows = iota((8, SLOTS), 0)
    return (
        jnp.where(rows == 1 + axis, scale, 0.0).astype(jnp.float32),
        jnp.where(rows == 4, scale, 0.0).astype(jnp.float32),
    )


def volume_body(a_ref, b_ref, tab, acc):
    for axis in range(3):
        normal_row, energy_row = flux_rows(axis, 1.0)
        stride = (36, 6, 1)[axis]

        def pencil(t, carry):
            base = (t, (t // 6) * 36 + t % 6, t * 6)[axis]
            flux_a, flux_b = [], []
            for j in range(6):
                n = base + j * stride
                where = pl.multiple_of((axis * NODES + n) * 8, 8)
                speed = row8(b_ref, where + 6)
                pressure = row8(b_ref, where + 5)
                flux_a.append(block(a_ref, n)[...] * speed)
                flux_b.append(
                    b_ref[pl.ds(where, 8), :] * speed
                    + pressure * (normal_row + energy_row * speed)
                )
            for i in range(6):
                n = base + i * stride
                if axis == 0:
                    sum_a = block(a_ref, n)[...]
                    sum_b = block(b_ref, n)[...]
                else:
                    sum_a = block(acc, n, 16)[...]
                    sum_b = block(acc, n, 16, 8)[...]
                for j in range(6):
                    factor = row8(tab, D0 + i * 6 + j)
                    sum_a = sum_a + factor * flux_a[j]
                    sum_b = sum_b + factor * flux_b[j]
                block(acc, n, 16)[...] = sum_a
                block(acc, n, 16, 8)[...] = sum_b
            return carry

        lax.fori_loop(0, FACE, pencil, 0)


def volume(a, b, tab):
    return pl.pallas_call(
        volume_body,
        out_shape=jax.ShapeDtypeStruct((NODES * 16, SLOTS), jnp.float32),
        name="volume",
    )(a, b, tab)


def gather_lanes(value, index):
    return jnp.take_along_axis(value, index, axis=1)


def finish_body(
    a_ref, b_ref, high, acc_in, tab, order, links, before, after, far_table,
    out, acc, far, own_mid, far_mid, pair,
):
    acc[...] = acc_in[...]
    ob = order[...]
    for face in range(6):
        axis, side = divmod(face, 2)
        sign = 0.5 if side else -0.5
        halo = after if side else before
        link = jnp.broadcast_to(links[pl.ds(face, 1), :], (8, SLOTS))
        outside = link >= BAND + SLOTS if side else link < BAND
        halo_lane = jnp.where(outside, link - (BAND + SLOTS if side else 0), 0)
        own_lane = jnp.clip(link - BAND, 0, SLOTS - 1)
        far_order = jnp.where(
            outside,
            gather_lanes(halo[pl.ds(HALO, 8), :], halo_lane),
            gather_lanes(ob, own_lane),
        )
        column = jnp.where(ob > 0.0, (ob - 1.0) * 5.0 + far_order - 1.0, -1.0)
        pick = (iota((128, SLOTS), 0).astype(jnp.float32) == column[0:1, :]).astype(jnp.float32)
        pair[...] = jnp.dot(
            far_table[...],
            pick,
            precision=lax.Precision.HIGHEST,
            preferred_element_type=jnp.float32,
        )

        def low_block(part, q):
            b, c = divmod(q, 6)
            n = node_of(axis, 0, b, c)
            if part == 0:
                return a_ref[pl.ds(n * 8, 8), :]
            return b_ref[pl.ds((axis * NODES + n) * 8, 8), :]

        def high_block(part, q):
            return high[pl.ds(((axis * FACE + q) * 2 + part) * 8, 8), :]

        inner, outer = (high_block, low_block) if side else (low_block, high_block)
        fastest = None
        for q in range(FACE):
            for part in range(2):
                word, k = divmod((axis * FACE + q) * 2 + part, 8)
                here = gather_lanes(outer(part, q), own_lane)
                there = gather_lanes(halo[pl.ds(word * 8, 8), :], halo_lane + 16 * k)
                value = jnp.where(outside, there, here)
                far[pl.ds((q * 2 + part) * 8, 8), :] = value
                if part == 1:
                    value = jnp.maximum(value, inner(1, q))
                    fastest = value if fastest is None else jnp.maximum(fastest, value)
        penalty = 0.5 * jnp.broadcast_to(fastest[7:8, :], (8, SLOTS))
        normal_row, energy_row = flux_rows(axis, sign)

        def weighted(block_a, ref_b, start):
            start = pl.multiple_of(start, 8)
            speed = row8(ref_b, start + 6)
            pressure = row8(ref_b, start + 5)
            mix = sign * speed - penalty
            return (
                block_a * mix,
                ref_b[pl.ds(start, 8), :] * mix + pressure * (normal_row + energy_row * speed),
            )

        def first(k, carry):
            for ours in (True, False):
                points = []
                for j in range(6):
                    if not ours:
                        start = (j * 6 + k) * 16
                        points.append(weighted(block(far, j * 6 + k, 16)[...], far, start + 8))
                    elif side:
                        index = axis * FACE + j * 6 + k
                        points.append(weighted(block(high, index, 16)[...], high, index * 16 + 8))
                    else:
                        n = node_of(axis, 0, j, k)
                        points.append(weighted(block(a_ref, n)[...], b_ref, (axis * NODES + n) * 8))
                table, offset, mid = (tab, M1, own_mid) if ours else (pair, 0, far_mid)
                for b in range(6):
                    for part in range(2):
                        total = None
                        for j in range(6):
                            term = row8(table, offset + b * 6 + j) * points[j][part]
                            total = term if total is None else total + term
                        block(mid, b * 6 + k, 16, 8 * part)[...] = total
            return carry

        def second(b, carry):
            for c in range(6):
                for part in range(2):
                    total = None
                    for k in range(6):
                        term = row8(tab, M2 + c * 6 + k) * block(own_mid, b * 6 + k, 16, 8 * part)[...]
                        term = term + row8(pair, 40 + c * 6 + k) * block(far_mid, b * 6 + k, 16, 8 * part)[...]
                        total = term if total is None else total + term
                    if side == 0:
                        place = block(acc, node_of(axis, 0, b, c), 16, 8 * part)
                        place[...] = place[...] + total
                    else:
                        for layer in range(1, 6):
                            place = block(acc, node_of(axis, layer, b, c), 16, 8 * part)
                            place[...] = place[...] + jnp.where(ob == float(layer), total, 0.0)
            return carry

        lax.fori_loop(0, 6, first, 0)
        lax.fori_loop(0, 6, second, 0)

    zero = jnp.zeros((8, SLOTS), jnp.float32)
    large = jnp.full((8, SLOTS), 1e30, jnp.float32)

    def reduce(t, carry):
        mean_a, mean_b, low_a, low_b = carry
        weight = row8(tab, W0 + t // 6) * row8(tab, W0 + t % 6)
        active = row8(tab, ACT + t // 6) * row8(tab, ACT + t % 6)
        for c in range(6):
            value_a = block(acc, t * 6 + c, 16)[...]
            value_b = block(acc, t * 6 + c, 16, 8)[...]
            here = weight * row8(tab, W0 + c)
            mask = active * row8(tab, ACT + c) > 0.0
            mean_a = mean_a + value_a * here
            mean_b = mean_b + value_b * here
            low_a = jnp.minimum(low_a, jnp.where(mask, value_a, 1e30))
            low_b = jnp.minimum(low_b, jnp.where(mask, value_b, 1e30))
        return mean_a, mean_b, low_a, low_b

    mean_a, mean_b, low_a, low_b = lax.fori_loop(0, FACE, reduce, (zero, zero, large, large))

    def limiter(mean, low):
        return jnp.minimum(
            1.0, jnp.maximum(mean - positivity_eps, 0.0) / jnp.maximum(mean - low, floor_gap)
        )

    scale_a, scale_b = limiter(mean_a, low_a), limiter(mean_b, low_b)
    is_species = iota((8, SLOTS), 0) == 0

    def write(t, carry):
        active = row8(tab, ACT + t // 6) * row8(tab, ACT + t % 6)
        for c in range(6):
            n = t * 6 + c
            value_a = block(acc, n, 16)[...]
            value_b = block(acc, n, 16, 8)[...]
            mask = active * row8(tab, ACT + c) > 0.0
            value_a = jnp.where(mask, mean_a + scale_a * (value_a - mean_a), 0.0)
            scaled = jnp.where(is_species, mean_b + scale_b * (value_b - mean_b), value_b)
            value_b = jnp.where(mask, scaled, 0.0)
            out[pl.ds(n, 8, stride=NODES), :] = value_a
            out[pl.ds(8 * NODES + n, 5, stride=NODES), :] = value_b[0:5, :]
        return carry

    lax.fori_loop(0, FACE, write, 0)


def finish(a, b, high, acc, tab, order, links, before, after, far_table):
    vmem = lambda rows: pltpu.VMEM((rows, SLOTS), jnp.float32)
    return pl.pallas_call(
        finish_body,
        out_shape=jax.ShapeDtypeStruct((NV * NODES, SLOTS), jnp.float32),
        scratch_shapes=[vmem(NODES * 16), vmem(FACE * 16), vmem(FACE * 16), vmem(FACE * 16), vmem(80)],
        name="finish",
    )(a, b, high, acc, tab, order, links, before, after, far_table)


def local(state_send, order_send, send_count, neighbours):
    peers = lax.axis_size(GROUP)
    capacity = SLOTS // peers
    chunk = capacity * lax.axis_size("gz")
    own_table, far_table = element_tables()
    state = state_send.reshape(NV * NODES, SLOTS)
    side = lax.axis_index("zh").reshape(1)
    own, away = pack(state, order_send, send_count, side, chunk)
    came = lax.ppermute(away, "zh", [(0, 1), (1, 0)])

    def spread(half):
        blocks = half.reshape(peers // 2, capacity * PITCH, 128)
        return lax.all_to_all(blocks, SIDE, split_axis=0, concat_axis=0, tiled=True)

    near_blocks = spread(own)
    away_blocks = spread(unpack(came, side, capacity, chunk))
    full = jnp.maximum(jnp.max(near_blocks[:, FLAG, 0]), jnp.max(away_blocks[:, FLAG, 0])) > 0.0

    def direct():
        packed = pack_all(state, order_send.reshape(1, SLOTS), send_count)
        blocks = packed.reshape(peers, capacity * PITCH, 128)
        moved = lax.all_to_all(blocks, GROUP, split_axis=0, concat_axis=0, tiled=True)
        moved = moved.reshape(
            lax.axis_size("y"), 2, lax.axis_size("gz"), capacity * PITCH, 128
        )
        halves = [
            lax.dynamic_index_in_dim(moved, which, 1, keepdims=False).reshape(near_blocks.shape)
            for which in (side[0], 1 - side[0])
        ]
        return halves[0], halves[1]

    near_blocks, away_blocks = lax.cond(full, direct, lambda: (near_blocks, away_blocks))
    a, b, high, up, down, tab, order = prep(
        near_blocks.reshape(HALF * PITCH, 128),
        away_blocks.reshape(HALF * PITCH, 128),
        own_table,
        side,
        chunk,
    )
    devices = lax.axis_size(AXES)
    forward = [(i, i + 1) for i in range(devices - 1)]
    before = lax.ppermute(up, AXES, forward)
    after = lax.ppermute(down, AXES, [(j, i) for i, j in forward])
    acc = volume(a, b, tab)
    result = finish(a, b, high, acc, tab, order, neighbours, before, after, far_table)
    return result.reshape(NV, NODES, SLOTS)


def solution(mesh):
    sizes = mesh.devices.shape
    parts = Mesh(mesh.devices.reshape(sizes[0], sizes[1] // 2, 2, sizes[2]), AXES)
    placed = (
        P(None, None, AXES),
        P(AXES),
        P(AXES, None),
        P(None, AXES),
    )
    return jax.shard_map(
        local,
        mesh=parts,
        in_specs=placed,
        out_specs=P(None, None, AXES),
        check_vma=False,
    )
```
